512 devices in a mesh: band: 8 (over z_lo, core), dom: 64 (over x, y, z_hi).
Axes of the slice: x: 4, y: 8, z: 8 (z_hi: 2, z_lo: 4; z = z_hi * 4 + z_lo), core: 2. Of those that a mesh axis runs over, the one named last changes fastest.
Arguments:
- orbitals: float32 [96, 128, 128, 128], P('band', 'dom'), may hold values from -6 to 6
- occupations: float32 [96], replicated, may hold values from 0.25 to 2
Outputs:
- exchange_terms: float32 [96, 128, 128, 128], P('band', 'dom')
The draws below stay inside these ranges and needn't reach their ends.
All inputs are finite; a program needn't handle non-finite values.
Results may differ from the reference program's by a relative error of at most 0.0001.
Values sent between devices are 32-bit elements; how exact they have to be, the bound alone decides.
A program may use at most 128 MiB of HBM per device.

```python
import math
import jax
import jax.numpy as jnp
from jax import lax

ORB_DEV = 12
BLOCK = 2
STEPS = 2
SWEEPS = 2
CY = 128
CZ = 128
NORB = 96
NX = 128
N_BAND = 8


def draw_orbitals(key, part):
    first_key = jax.random.fold_in(key, 0)
    rough_part = jnp.clip(jax.random.normal(first_key, (NORB, NX, CY, CZ), jnp.float32), -4.0, 4.0)
    return rough_part


def setup_inputs(seed: int = 0) -> dict:
    keys = jax.random.split(jax.random.key(seed), 3)
    orbitals = draw_orbitals(jax.random.fold_in(keys[2], 71), 0)
    occupations = jnp.clip(jnp.exp(jax.random.uniform(keys[1], (NORB,), jnp.float32, math.log(0.25), math.log(2.0))), 0.25, 2.0)
    return dict(orbitals=orbitals, occupations=occupations)


def neighbours(field):
    lead = field.ndim - 3
    padded = jnp.pad(field, [(0, 0)] * lead + [(1, 1)] * 3)
    total = padded[..., 2:, 1:-1, 1:-1] + padded[..., :-2, 1:-1, 1:-1]
    total = total + padded[..., 1:-1, 2:, 1:-1] + padded[..., 1:-1, :-2, 1:-1]
    total = total + padded[..., 1:-1, 1:-1, 2:] + padded[..., 1:-1, 1:-1, :-2]
    return total


def solve_potential(density):
    potential = density / 6.0
    for sweep_index in range(SWEEPS):
        potential = (density + neighbours(potential)) / 6.0
    return potential


def reference(orbitals, occupations):
    exchange_terms = jnp.zeros(orbitals.shape, jnp.float32)
    for step_index in range(STEPS):
        owner = step_index * (N_BAND // STEPS)
        first = owner * ORB_DEV + step_index * BLOCK
        owner_block = orbitals[first:first + BLOCK]
        weights = occupations[first:first + BLOCK]

        def per_orbital(target):
            density = owner_block * target[None]
            potential = solve_potential(density)
            step_sum = jnp.zeros(target.shape, jnp.float32)
            for block_index in range(BLOCK):
                step_sum = step_sum - weights[block_index] * potential[block_index] * owner_block[block_index]
            return step_sum

        exchange_terms = exchange_terms + lax.map(per_orbital, orbitals)
    return exchange_terms
```

```python
import functools

import jax
import jax.numpy as jnp
from jax import lax
from jax.experimental import pallas as pl
from jax.experimental.pallas import tpu as pltpu
from jax.sharding import PartitionSpec as P

MESH = pl.DeviceIdType.MESH

BLOCK = 2
STEPS = 2
NB = BLOCK * STEPS
CY = 128
CZ = 128
SLAB = 2 * CY
PAIRS = 32
HALF = 6
STRIP = 8

PLANE_OFFSETS = [
    (dx, dy) for dx in range(-2, 3) for dy in range(-2, 3) if abs(dx) + abs(dy) <= 2
]
OFFSETS = [
    (dx, dy, dz)
    for dx, dy in PLANE_OFFSETS
    for dz in range(-2, 3)
    if abs(dx) + abs(dy) + abs(dz) <= 2
]
INDEX = {offset: k for k, offset in enumerate(OFFSETS)}


def coefficient(offset):
    steps = sum(abs(d) for d in offset)
    if steps == 1:
        return 1.0 / 36.0
    return (1.0 if 2 in map(abs, offset) else 2.0) / 216.0


def kernel(
    weight_rows,
    occ_ref,
    x_ref,
    o_ref,
    w_ref,
    block_ref,
    k_ref,
    out_ref,
    own_sem,
    cross_send,
    cross_recv,
    direct_send,
    direct_recv,
    pass_send,
    pass_recv,
    back_send,
    back_recv,
    keep_sem,
    root_send,
    root_recv,
    root_own,
    side_send,
    side_recv,
    core_send,
    core_recv,
):
    band, dom = lax.axis_index("band"), lax.axis_index("dom")
    core, z_lo = lax.rem(band, 2), band // 2
    half, pair = lax.rem(dom, 2), dom // 2
    right_pair = lax.rem(pair + 1, PAIRS)
    left_pair = lax.rem(pair + PAIRS - 1, PAIRS)
    partner = (band, dom + 1 - 2 * half)
    sibling = (band + 1 - 2 * core, dom)
    right = (band, 2 * right_pair + half)
    left = (band, 2 * left_pair + half)
    ahead = (band, 2 * jnp.where(half == 0, right_pair, left_pair) + half)
    behind = (band, 2 * jnp.where(half == 0, left_pair, right_pair) + half)
    first_root = band == 0
    second_root = band == 4

    def rows(slab):
        return pl.ds(pl.multiple_of(slab * SLAB, SLAB), SLAB)

    def remote(src, dst, send, recv, device):
        return pltpu.make_async_remote_copy(
            src_ref=src,
            dst_ref=dst,
            send_sem=send,
            recv_sem=recv,
            device_id=device,
            device_id_type=MESH,
        )

    def own(i):
        return pltpu.make_async_copy(
            x_ref.at[HALF * half + i], w_ref.at[i, rows(1 + half)], own_sem.at[i]
        )

    def cross(i):
        return remote(
            x_ref.at[HALF * (1 - half) + i],
            w_ref.at[i, rows(1 + half)],
            cross_send.at[i],
            cross_recv.at[i],
            partner,
        )

    def direct(i):
        return remote(
            x_ref.at[HALF * half + i],
            w_ref.at[i, rows(3 - 3 * half)],
            direct_send.at[i],
            direct_recv.at[i],
            behind,
        )

    def passed(i):
        return remote(
            w_ref.at[i, rows(2 - half)],
            w_ref.at[i, rows(3 * half)],
            pass_send.at[i],
            pass_recv.at[i],
            ahead,
        )

    def back(i):
        return remote(
            out_ref.at[i, rows(1 - half)],
            o_ref.at[HALF * half + i],
            back_send.at[i],
            back_recv.at[i],
            partner,
        )

    def keep(i):
        return pltpu.make_async_copy(
            out_ref.at[i, rows(half)], o_ref.at[HALF * half + i], keep_sem.at[i]
        )

    def root(group, t, device):
        return remote(
            x_ref.at[pl.ds(BLOCK * group, BLOCK)],
            block_ref.at[pl.ds(BLOCK * group, BLOCK), rows(1 + half)],
            root_send.at[t],
            root_recv.at[half],
            device,
        )

    def root_arrival(slab):
        return remote(
            x_ref.at[pl.ds(BLOCK * core, BLOCK)],
            block_ref.at[pl.ds(BLOCK * core, BLOCK), rows(1 + slab)],
            root_send.at[0],
            root_recv.at[slab],
            sibling,
        )

    def root_local():
        return pltpu.make_async_copy(
            x_ref.at[pl.ds(0, BLOCK)],
            block_ref.at[pl.ds(0, BLOCK), rows(1 + half)],
            root_own,
        )

    mine = pl.ds(BLOCK * core, BLOCK)

    def side(t):
        return remote(
            block_ref.at[mine, rows(1 + t)],
            block_ref.at[mine, rows(3 - 3 * t)],
            side_send.at[t],
            side_recv.at[t],
            right if t else left,
        )

    def swap(t):
        part = (pl.ds(SLAB, 2 * SLAB), pl.ds(3 * SLAB, SLAB), pl.ds(0, SLAB))[t]
        return remote(
            block_ref.at[mine, part],
            block_ref.at[mine, part],
            core_send.at[t],
            core_recv.at[t],
            sibling,
        )

    def chip(k, c):
        return (2 * lax.rem(k, 4) + c, 2 * pair + k // 4)

    barrier = pltpu.get_barrier_semaphore()
    for device in (partner, sibling, left, right):
        pl.semaphore_signal(barrier, inc=1, device_id=device, device_id_type=MESH)

    my_chip = 4 * half + z_lo
    for slab in range(2):
        target = (4 * core, 2 * pair + slab)

        @pl.when(jnp.logical_or(band != 4 * core, half != slab))
        def _():
            pl.semaphore_signal(barrier, inc=1, device_id=target, device_id_type=MESH)

    @pl.when(jnp.logical_not(jnp.logical_or(first_root, second_root)))
    def _():
        pl.semaphore_wait(barrier, 4)

    @pl.when(first_root)
    def _():
        pl.semaphore_wait(barrier, 4 + 7)
        for t in range(1, 8):
            root(0, t, chip(lax.rem(my_chip + t, 8), 0)).start()
        root_local().start()

    @pl.when(second_root)
    def _():
        pl.semaphore_wait(barrier, 4 + 8)
        for t in range(8):
            root(1, t, chip(lax.rem(my_chip + t, 8), 1)).start()

    def begin(i, carry):
        cross(i).start()
        direct(i).start()
        own(i).start()
        return carry

    lax.fori_loop(0, HALF, begin, 0)

    for slab in range(2):
        local = jnp.logical_and(first_root, half == slab)

        @pl.when(local)
        def _():
            root_local().wait()

        @pl.when(jnp.logical_not(local))
        def _():
            root_arrival(slab).wait_recv()

    for t in range(2):
        side(t).start()
    swap(0).start()

    cross(0).wait_recv()
    passed(0).start()

    side(0).wait_recv()
    swap(1).start()
    side(1).wait_recv()
    swap(2).start()
    for t in range(3):
        swap(t).wait_recv()

    lane = lax.broadcasted_iota(jnp.int32, (STRIP, CZ), 1)
    sub = lax.broadcasted_iota(jnp.int32, (STRIP, CZ), 0)

    def stencil(r, carry):
        plane, y = 4 * pair + r // (CY // STRIP), sub + STRIP * lax.rem(
            r, CY // STRIP
        )
        start = SLAB + r * STRIP
        centre = []
        for b in range(NB):
            c = block_ref[b, pl.ds(start, STRIP), :] * (-occ_ref[weight_rows[b]])
            rolled = {}
            for dz in range(-2, 3):
                if dz == 0:
                    rolled[dz] = c
                else:
                    inside = lane >= dz if dz > 0 else lane < CZ + dz
                    rolled[dz] = jnp.where(
                        inside, pltpu.roll(c, dz % CZ, axis=1), 0.0
                    )
            centre.append(rolled)
        one, nil = jnp.float32(1.0), jnp.float32(0.0)
        for dx, dy in PLANE_OFFSETS:
            there = [
                block_ref[b, pl.ds(start + dx * CY + dy, STRIP), :] for b in range(NB)
            ]
            inside_x = jnp.logical_and(plane + dx >= 0, plane + dx < 4 * PAIRS)
            for dz in range(-2, 3):
                if abs(dx) + abs(dy) + abs(dz) > 2:
                    continue
                total = centre[0][dz] * there[0]
                for b in range(1, NB):
                    total = total + centre[b][dz] * there[b]
                if dx == dy == dz == 0:
                    sides = jnp.where(plane > 0, one, nil) + jnp.where(
                        plane < 4 * PAIRS - 1, one, nil
                    )
                    count = (
                        sides
                        + jnp.where(y > 0, one, nil)
                        + jnp.where(y < CY - 1, one, nil)
                        + jnp.where(lane > 0, one, nil)
                        + jnp.where(lane < CZ - 1, one, nil)
                    )
                    factor = (36.0 + count) * (1.0 / 216.0)
                else:
                    factor = jnp.float32(coefficient((dx, dy, dz)))
                    if dx:
                        factor = jnp.where(inside_x, factor, nil)
                    if dy:
                        inside_y = y + dy >= 0 if dy < 0 else y + dy < CY
                        factor = jnp.where(inside_y, factor, nil)
                k_ref[INDEX[dx, dy, dz], pl.ds(r * STRIP, STRIP), :] = total * factor
        return carry

    lax.fori_loop(0, 4 * CY // STRIP, stencil, 0)

    def orbital(i, carry):
        @pl.when(i + 1 < HALF)
        def _():
            cross(i + 1).wait_recv()
            passed(i + 1).start()

        own(i).wait()
        direct(i).wait_recv()
        passed(i).wait_recv()

        def strip(r, inner):
            start = SLAB + r * STRIP
            sums = {}
            for dx, dy in PLANE_OFFSETS:
                there = w_ref[i, pl.ds(start + dx * CY + dy, STRIP), :]
                for dz in range(-2, 3):
                    if abs(dx) + abs(dy) + abs(dz) <= 2:
                        term = k_ref[INDEX[dx, dy, dz], pl.ds(r * STRIP, STRIP), :] * there
                        sums[dz] = term if dz not in sums else sums[dz] + term
            result = sums[0]
            for dz in (-2, -1, 1, 2):
                result = result + pltpu.roll(sums[dz], -dz % CZ, axis=1)
            out_ref[i, pl.ds(r * STRIP, STRIP), :] = result
            return inner

        lax.fori_loop(0, 4 * CY // STRIP, strip, 0)
        back(i).start()
        keep(i).start()
        return carry

    lax.fori_loop(0, HALF, orbital, 0)

    def finish(i, carry):
        cross(i).wait_send()
        direct(i).wait_send()
        passed(i).wait_send()
        keep(i).wait()
        back(i).wait()
        return carry

    lax.fori_loop(0, HALF, finish, 0)
    for t in range(2):
        side(t).wait_send()
    for t in range(3):
        swap(t).wait_send()

    @pl.when(first_root)
    def _():
        for t in range(1, 8):
            root(0, t, chip(lax.rem(my_chip + t, 8), 0)).wait_send()

    @pl.when(second_root)
    def _():
        for t in range(8):
            root(1, t, chip(lax.rem(my_chip + t, 8), 1)).wait_send()


def per_device(orbitals, occupations):
    count, planes = orbitals.shape[:2]
    groups = lax.axis_size("band")
    weight_rows = [
        s * (groups // STEPS) * count + s * BLOCK + b
        for s in range(STEPS)
        for b in range(BLOCK)
    ]
    dma = pltpu.SemaphoreType.DMA
    out = pl.pallas_call(
        functools.partial(kernel, weight_rows),
        name="exchange",
        out_shape=jax.ShapeDtypeStruct((count, planes * CY, CZ), jnp.float32),
        in_specs=[
            pl.BlockSpec(memory_space=pltpu.SMEM),
            pl.BlockSpec(memory_space=pl.ANY),
        ],
        out_specs=pl.BlockSpec(memory_space=pl.ANY),
        scratch_shapes=[
            pltpu.VMEM((HALF, 4 * SLAB, CZ), jnp.float32),
            pltpu.VMEM((NB, 4 * SLAB, CZ), jnp.float32),
            pltpu.VMEM((len(OFFSETS), 2 * SLAB, CZ), jnp.float32),
            pltpu.VMEM((HALF, 2 * SLAB, CZ), jnp.float32),
            dma((HALF,)),
            dma((HALF,)),
            dma((HALF,)),
            dma((HALF,)),
            dma((HALF,)),
            dma((HALF,)),
            dma((HALF,)),
            dma((HALF,)),
            dma((HALF,)),
            dma((HALF,)),
            dma((8,)),
            dma((2,)),
            dma,
            dma((2,)),
            dma((2,)),
            dma((3,)),
            dma((3,)),
        ],
        compiler_params=pltpu.CompilerParams(
            collective_id=0, has_side_effects=True, vmem_limit_bytes=40 * 2**20
        ),
    )(occupations, orbitals.reshape(count, planes * CY, CZ))
    return out.reshape(orbitals.shape)


def solution(mesh):
    in_specs = (P("band", "dom", None, None), P())
    out_specs = P("band", "dom", None, None)
    return jax.shard_map(
        per_device, mesh=mesh, in_specs=in_specs, out_specs=out_specs, check_vma=False
    )
```

```python
import functools

import jax
import jax.numpy as jnp
from jax import lax
from jax.experimental import pallas as pl
from jax.experimental.pallas import tpu as pltpu
from jax.sharding import PartitionSpec as P

MESH = pl.DeviceIdType.MESH

BLOCK = 2
STEPS = 2
NB = BLOCK * STEPS
CY = 128
CZ = 128
SLAB = 2 * CY
PAIRS = 32
HALF = 6
STRIP = 128
KSTRIP = 64
EARLY = 3
RELAYS = (1, 2, -1, -2)
SEEDS = (*RELAYS, 0)
WINDOW = 3

PLANE_OFFSETS = [
    (dx, dy) for dx in range(-2, 3) for dy in range(-2, 3) if abs(dx) + abs(dy) <= 2
]
OFFSETS = [
    (dx, dy, dz)
    for dx, dy in PLANE_OFFSETS
    for dz in range(-2, 3)
    if abs(dx) + abs(dy) + abs(dz) <= 2
]
INDEX = {offset: k for k, offset in enumerate(OFFSETS)}


def coefficient(offset):
    steps = sum(abs(d) for d in offset)
    if steps == 1:
        return 1.0 / 36.0
    return (1.0 if 2 in map(abs, offset) else 2.0) / 216.0


def kernel(
    weight_rows,
    occ_hbm,
    x_ref,
    o_ref,
    occ_ref,
    occ_sem,
    w_ref,
    block_ref,
    k_ref,
    out_ref,
    own_sem,
    cross_send,
    cross_recv,
    direct_send,
    direct_recv,
    pass_send,
    pass_recv,
    back_send,
    back_recv,
    keep_sem,
    root_own,
    seed_send,
    relay_send,
    root_recv,
    side_send,
    side_recv,
    core_send,
    core_recv,
):
    band, dom = lax.axis_index("band"), lax.axis_index("dom")
    core, z_lo = lax.rem(band, 2), band // 2
    half, pair = lax.rem(dom, 2), dom // 2
    right_pair = lax.rem(pair + 1, PAIRS)
    left_pair = lax.rem(pair + PAIRS - 1, PAIRS)
    partner = (band, dom + 1 - 2 * half)
    sibling = (band + 1 - 2 * core, dom)
    right = (band, 2 * right_pair + half)
    left = (band, 2 * left_pair + half)
    ahead = (band, 2 * jnp.where(half == 0, right_pair, left_pair) + half)
    behind = (band, 2 * jnp.where(half == 0, left_pair, right_pair) + half)
    z = 4 * half + z_lo

    def chip(step, c):
        k = lax.rem(z + step + 8, 8)
        return (2 * lax.rem(k, 4) + c, 2 * pair + k // 4)

    def rows(slab):
        return pl.ds(pl.multiple_of(slab * SLAB, SLAB), SLAB)

    def remote(src, dst, send, recv, device):
        return pltpu.make_async_remote_copy(
            src_ref=src,
            dst_ref=dst,
            send_sem=send,
            recv_sem=recv,
            device_id=device,
            device_id_type=MESH,
        )

    def own(i):
        return pltpu.make_async_copy(
            x_ref.at[HALF * half + i], w_ref.at[i, rows(1 + half)], own_sem.at[i]
        )

    def cross(i):
        return remote(
            x_ref.at[HALF * (1 - half) + i],
            w_ref.at[i, rows(1 + half)],
            cross_send.at[i],
            cross_recv.at[i],
            partner,
        )

    def direct(i):
        return remote(
            x_ref.at[HALF * half + i],
            w_ref.at[i, rows(3 - 3 * half)],
            direct_send.at[i],
            direct_recv.at[i],
            behind,
        )

    def passed(i):
        return remote(
            w_ref.at[i, rows(2 - half)],
            w_ref.at[i, rows(3 * half)],
            pass_send.at[i],
            pass_recv.at[i],
            ahead,
        )

    def back(i):
        return remote(
            out_ref.at[i, rows(1 - half)],
            o_ref.at[HALF * half + i],
            back_send.at[i],
            back_recv.at[i],
            partner,
        )

    def keep(i):
        return pltpu.make_async_copy(
            out_ref.at[i, rows(half)], o_ref.at[HALF * half + i], keep_sem.at[i]
        )

    mine = pl.ds(BLOCK * core, BLOCK)
    is_root = jnp.logical_or(band == 0, band == 4)
    group = band // 4
    is_relay = jnp.logical_and(lax.rem(z, 2) == 0, lax.rem(z, 4) != 2 * core)
    before = lax.rem(z + 6, 8) // 4

    def seed(u, step):
        return remote(
            x_ref.at[BLOCK * group + u],
            block_ref.at[BLOCK * group + u, rows(1 + half)],
            seed_send.at[u, SEEDS.index(step)],
            root_recv.at[half, u],
            sibling if step == 0 else chip(step, group),
        )

    def seed_local(u):
        return pltpu.make_async_copy(
            x_ref.at[u], block_ref.at[u, rows(1 + half)], root_own.at[u]
        )

    def relay(slab, u, step):
        part = block_ref.at[BLOCK * core + u, rows(1 + slab)]
        return remote(
            part,
            part,
            relay_send.at[u, RELAYS.index(step)],
            root_recv.at[slab, u],
            chip(step, core),
        )

    def relays(u, act):
        act(relay(before, u, 1))
        if u == 0:
            act(relay(before, u, 2))
        act(relay(1 - before, u, -1))
        if u == 1:
            act(relay(1 - before, u, -2))

    def arrive(u):
        @pl.when(is_relay)
        def _():
            for slab in range(2):
                relay(slab, u, 1).wait_recv()
            relays(u, lambda copy: copy.start())

        for slab in range(2):
            local = jnp.logical_and(band == 0, half == slab)

            @pl.when(local)
            def _():
                seed_local(u).wait()

            @pl.when(jnp.logical_not(jnp.logical_or(local, is_relay)))
            def _():
                relay(slab, u, 1).wait_recv()

    def side(slab):
        return remote(
            block_ref.at[mine, rows(1 + slab)],
            block_ref.at[mine, rows(3 - 3 * slab)],
            side_send.at[slab],
            side_recv.at[slab],
            (band, 2 * jnp.where(slab == 0, left_pair, right_pair) + half),
        )

    def swap(slot):
        part = block_ref.at[mine, rows(slot)]
        return remote(part, part, core_send.at[slot], core_recv.at[slot], sibling)

    weights = pltpu.make_async_copy(occ_hbm, occ_ref, occ_sem)
    weights.start()

    barrier = pltpu.get_barrier_semaphore()
    near = [chip(step, c) for step in RELAYS for c in range(2)]
    for device in (partner, sibling, left, right, *near):
        pl.semaphore_signal(barrier, inc=1, device_id=device, device_id_type=MESH)
    pl.semaphore_wait(barrier, 4 + len(near))

    @pl.when(band == 0)
    def _():
        for u in range(BLOCK):
            seed_local(u).start()

    @pl.when(band == 4)
    def _():
        for u in range(BLOCK):
            seed(u, 0).start()

    @pl.when(is_root)
    def _():
        for steps in ((2, -2), (1, -1)):
            for u in range(BLOCK):
                for step in steps:
                    seed(u, step).start()

    for i in range(EARLY):
        direct(i).start()
    for i in range(HALF):
        own(i).start()

    def advance(i):
        cross(i).wait_recv()
        passed(i).start()

        @pl.when(i + WINDOW < HALF)
        def _():
            cross(i + WINDOW).start()

        @pl.when(i + EARLY < HALF)
        def _():
            direct(i + EARLY).start()

    for u in range(BLOCK):
        arrive(u)
    for slab in range(2):
        side(slab).start()
        swap(1 + slab).start()
    for i in range(WINDOW):
        cross(i).start()
    advance(0)
    for slab in range(2):
        side(slab).wait_recv()
        swap(3 - 3 * slab).start()
    for slot in range(4):
        swap(slot).wait_recv()

    weights.wait()
    lane = lax.broadcasted_iota(jnp.int32, (KSTRIP, CZ), 1)
    sub = lax.broadcasted_iota(jnp.int32, (KSTRIP, CZ), 0)

    def stencil(r, carry):
        plane, y = 4 * pair + r // (CY // KSTRIP), sub + KSTRIP * lax.rem(
            r, CY // KSTRIP
        )
        start = SLAB + r * KSTRIP
        centre = []
        for b in range(NB):
            c = block_ref[b, pl.ds(start, KSTRIP), :] * (-occ_ref[weight_rows[b]])
            rolled = {}
            for dz in range(-2, 3):
                if dz == 0:
                    rolled[dz] = c
                else:
                    inside = lane >= dz if dz > 0 else lane < CZ + dz
                    rolled[dz] = jnp.where(
                        inside, pltpu.roll(c, dz % CZ, axis=1), 0.0
                    )
            centre.append(rolled)
        one, nil = jnp.float32(1.0), jnp.float32(0.0)
        for dx, dy in PLANE_OFFSETS:
            there = [
                block_ref[b, pl.ds(start + dx * CY + dy, KSTRIP), :] for b in range(NB)
            ]
            inside_x = jnp.logical_and(plane + dx >= 0, plane + dx < 4 * PAIRS)
            for dz in range(-2, 3):
                if abs(dx) + abs(dy) + abs(dz) > 2:
                    continue
                total = centre[0][dz] * there[0]
                for b in range(1, NB):
                    total = total + centre[b][dz] * there[b]
                if dx == dy == dz == 0:
                    sides = jnp.where(plane > 0, one, nil) + jnp.where(
                        plane < 4 * PAIRS - 1, one, nil
                    )
                    count = (
                        sides
                        + jnp.where(y > 0, one, nil)
                        + jnp.where(y < CY - 1, one, nil)
                        + jnp.where(lane > 0, one, nil)
                        + jnp.where(lane < CZ - 1, one, nil)
                    )
                    factor = (36.0 + count) * (1.0 / 216.0)
                else:
                    factor = jnp.float32(coefficient((dx, dy, dz)))
                    if dx:
                        factor = jnp.where(inside_x, factor, nil)
                    if dy:
                        inside_y = y + dy >= 0 if dy < 0 else y + dy < CY
                        factor = jnp.where(inside_y, factor, nil)
                k_ref[INDEX[dx, dy, dz], pl.ds(r * KSTRIP, KSTRIP), :] = total * factor
        return carry

    lax.fori_loop(0, 4 * CY // KSTRIP, stencil, 0)

    def orbital(i, carry):
        @pl.when(i + 1 < HALF)
        def _():
            advance(i + 1)

        own(i).wait()
        direct(i).wait_recv()
        passed(i).wait_recv()

        def strip(r, inner):
            start = SLAB + r * STRIP
            sums = {}
            for dx, dy in PLANE_OFFSETS:
                there = w_ref[i, pl.ds(start + dx * CY + dy, STRIP), :]
                for dz in range(-2, 3):
                    if abs(dx) + abs(dy) + abs(dz) <= 2:
                        term = k_ref[INDEX[dx, dy, dz], pl.ds(r * STRIP, STRIP), :] * there
                        sums[dz] = term if dz not in sums else sums[dz] + term
            result = sums[0]
            for dz in (-2, -1, 1, 2):
                result = result + pltpu.roll(sums[dz], -dz % CZ, axis=1)
            out_ref[i, pl.ds(r * STRIP, STRIP), :] = result
            return inner

        def planes(slab):
            first = slab * (SLAB // STRIP)
            lax.fori_loop(first, first + SLAB // STRIP, strip, 0)

        planes(1 - half)
        back(i).start()
        planes(half)
        keep(i).start()
        return carry

    lax.fori_loop(0, HALF, orbital, 0)

    def finish(i, carry):
        cross(i).wait_send()
        direct(i).wait_send()
        passed(i).wait_send()
        keep(i).wait()
        back(i).wait()
        return carry

    lax.fori_loop(0, HALF, finish, 0)
    for slab in range(2):
        side(slab).wait_send()
    for slot in range(4):
        swap(slot).wait_send()

    @pl.when(is_relay)
    def _():
        for u in range(BLOCK):
            relays(u, lambda copy: copy.wait_send())

    @pl.when(band == 4)
    def _():
        for u in range(BLOCK):
            seed(u, 0).wait_send()

    @pl.when(is_root)
    def _():
        for u in range(BLOCK):
            for step in RELAYS:
                seed(u, step).wait_send()


def per_device(orbitals, occupations):
    count, planes = orbitals.shape[:2]
    groups = lax.axis_size("band")
    weight_rows = [
        s * (groups // STEPS) * count + s * BLOCK + b
        for s in range(STEPS)
        for b in range(BLOCK)
    ]
    dma = pltpu.SemaphoreType.DMA
    out = pl.pallas_call(
        functools.partial(kernel, weight_rows),
        name="exchange",
        out_shape=jax.ShapeDtypeStruct((count, planes * CY, CZ), jnp.float32),
        in_specs=[
            pl.BlockSpec(memory_space=pltpu.HBM),
            pl.BlockSpec(memory_space=pltpu.HBM),
        ],
        out_specs=pl.BlockSpec(memory_space=pl.ANY),
        scratch_shapes=[
            pltpu.SMEM(occupations.shape, jnp.float32),
            dma,
            pltpu.VMEM((HALF, 4 * SLAB, CZ), jnp.float32),
            pltpu.VMEM((NB, 4 * SLAB, CZ), jnp.float32),
            pltpu.VMEM((len(OFFSETS), 2 * SLAB, CZ), jnp.float32),
            pltpu.VMEM((HALF, 2 * SLAB, CZ), jnp.float32),
            dma((HALF,)),
            dma((HALF,)),
            dma((HALF,)),
            dma((HALF,)),
            dma((HALF,)),
            dma((HALF,)),
            dma((HALF,)),
            dma((HALF,)),
            dma((HALF,)),
            dma((HALF,)),
            dma((BLOCK,)),
            dma((BLOCK, len(SEEDS))),
            dma((BLOCK, len(RELAYS))),
            dma((2, BLOCK)),
            dma((2,)),
            dma((2,)),
            dma((4,)),
            dma((4,)),
        ],
        compiler_params=pltpu.CompilerParams(
            collective_id=0, has_side_effects=True, vmem_limit_bytes=40 * 2**20
        ),
    )(occupations, orbitals.reshape(count, planes * CY, CZ))
    return out.reshape(orbitals.shape)


def solution(mesh):
    in_specs = (P("band", "dom", None, None), P())
    out_specs = P("band", "dom", None, None)
    return jax.shard_map(
        per_device, mesh=mesh, in_specs=in_specs, out_specs=out_specs, check_vma=False
    )
```

```python
import functools

import jax
import jax.numpy as jnp
from jax import lax
from jax.experimental import pallas as pl
from jax.experimental.pallas import tpu as pltpu
from jax.sharding import PartitionSpec as P

MESH = pl.DeviceIdType.MESH

BLOCK = 2
STEPS = 2
NB = BLOCK * STEPS
CY = 128
CZ = 128
SLAB = 2 * CY
PAIRS = 32
HALF = 6
STRIP = 128
KSTRIP = 64
EARLY = 3
RELAYS = (1, 2, -1, -2)
SEEDS = (*RELAYS, 0)
WINDOW = 3

PLANE_OFFSETS = [
    (dx, dy) for dx in range(-2, 3) for dy in range(-2, 3) if abs(dx) + abs(dy) <= 2
]
OFFSETS = [
    (dx, dy, dz)
    for dx, dy in PLANE_OFFSETS
    for dz in range(-2, 3)
    if abs(dx) + abs(dy) + abs(dz) <= 2
]
INDEX = {offset: k for k, offset in enumerate(OFFSETS)}


def coefficient(offset):
    steps = sum(abs(d) for d in offset)
    if steps == 1:
        return 1.0 / 36.0
    return (1.0 if 2 in map(abs, offset) else 2.0) / 216.0


def kernel(
    weight_rows,
    occ_hbm,
    x_ref,
    o_ref,
    occ_ref,
    occ_sem,
    w_ref,
    block_ref,
    k_ref,
    out_ref,
    own_sem,
    cross_send,
    cross_recv,
    direct_send,
    direct_recv,
    pass_send,
    pass_recv,
    back_send,
    back_recv,
    keep_sem,
    root_own,
    seed_send,
    relay_send,
    root_recv,
    side_send,
    side_recv,
    core_send,
    core_recv,
):
    band, dom = lax.axis_index("band"), lax.axis_index("dom")
    core, z_lo = lax.rem(band, 2), band // 2
    half, pair = lax.rem(dom, 2), dom // 2
    right_pair = lax.rem(pair + 1, PAIRS)
    left_pair = lax.rem(pair + PAIRS - 1, PAIRS)
    partner = (band, dom + 1 - 2 * half)
    sibling = (band + 1 - 2 * core, dom)
    right = (band, 2 * right_pair + half)
    left = (band, 2 * left_pair + half)
    ahead = (band, 2 * jnp.where(half == 0, right_pair, left_pair) + half)
    behind = (band, 2 * jnp.where(half == 0, left_pair, right_pair) + half)
    z = 4 * half + z_lo

    def chip(step, c):
        k = lax.rem(z + step + 8, 8)
        return (2 * lax.rem(k, 4) + c, 2 * pair + k // 4)

    def rows(slab):
        return pl.ds(pl.multiple_of(slab * SLAB, SLAB), SLAB)

    def remote(src, dst, send, recv, device):
        return pltpu.make_async_remote_copy(
            src_ref=src,
            dst_ref=dst,
            send_sem=send,
            recv_sem=recv,
            device_id=device,
            device_id_type=MESH,
        )

    def own(i):
        return pltpu.make_async_copy(
            x_ref.at[HALF * half + i], w_ref.at[i, rows(1 + half)], own_sem.at[i]
        )

    def cross(i):
        return remote(
            x_ref.at[HALF * (1 - half) + i],
            w_ref.at[i, rows(1 + half)],
            cross_send.at[i],
            cross_recv.at[i],
            partner,
        )

    def direct(i):
        return remote(
            x_ref.at[HALF * half + i],
            w_ref.at[i, rows(3 - 3 * half)],
            direct_send.at[i],
            direct_recv.at[i],
            behind,
        )

    def passed(i):
        return remote(
            w_ref.at[i, rows(2 - half)],
            w_ref.at[i, rows(3 * half)],
            pass_send.at[i],
            pass_recv.at[i],
            ahead,
        )

    def back(i):
        return remote(
            out_ref.at[i, rows(1 - half)],
            o_ref.at[HALF * half + i],
            back_send.at[i],
            back_recv.at[i],
            partner,
        )

    def keep(i):
        return pltpu.make_async_copy(
            out_ref.at[i, rows(half)], o_ref.at[HALF * half + i], keep_sem.at[i]
        )

    mine = pl.ds(BLOCK * core, BLOCK)
    is_root = jnp.logical_or(band == 0, band == 4)
    group = band // 4
    is_relay = jnp.logical_and(lax.rem(z, 2) == 0, lax.rem(z, 4) != 2 * core)
    before = lax.rem(z + 6, 8) // 4

    def seed(u, step):
        return remote(
            x_ref.at[BLOCK * group + u],
            block_ref.at[BLOCK * group + u, rows(1 + half)],
            seed_send.at[u, SEEDS.index(step)],
            root_recv.at[half, u],
            sibling if step == 0 else chip(step, group),
        )

    def seed_local(u):
        return pltpu.make_async_copy(
            x_ref.at[u], block_ref.at[u, rows(1 + half)], root_own.at[u]
        )

    def relay(slab, u, step):
        part = block_ref.at[BLOCK * core + u, rows(1 + slab)]
        return remote(
            part,
            part,
            relay_send.at[u, RELAYS.index(step)],
            root_recv.at[slab, u],
            chip(step, core),
        )

    def relays(u, act):
        if u == 0:
            act(relay(before, u, 2))
        else:
            act(relay(1 - before, u, -2))
        act(relay(1 - before, u, -1))
        act(relay(before, u, 1))

    def arrive(u):
        @pl.when(is_relay)
        def _():
            for slab in range(2):
                relay(slab, u, 1).wait_recv()
            relays(u, lambda copy: copy.start())

        for slab in range(2):
            local = jnp.logical_and(band == 0, half == slab)

            @pl.when(local)
            def _():
                seed_local(u).wait()

            @pl.when(jnp.logical_not(jnp.logical_or(local, is_relay)))
            def _():
                relay(slab, u, 1).wait_recv()

    def side(slab):
        return remote(
            block_ref.at[mine, rows(1 + slab)],
            block_ref.at[mine, rows(3 - 3 * slab)],
            side_send.at[slab],
            side_recv.at[slab],
            (band, 2 * jnp.where(slab == 0, left_pair, right_pair) + half),
        )

    def swap(slot):
        part = block_ref.at[mine, rows(slot)]
        return remote(part, part, core_send.at[slot], core_recv.at[slot], sibling)

    weights = pltpu.make_async_copy(occ_hbm, occ_ref, occ_sem)
    weights.start()

    barrier = pltpu.get_barrier_semaphore()
    near = [chip(step, c) for step in RELAYS for c in range(2)]
    for device in (partner, sibling, left, right, *near):
        pl.semaphore_signal(barrier, inc=1, device_id=device, device_id_type=MESH)
    pl.semaphore_wait(barrier, 4 + len(near))

    @pl.when(band == 0)
    def _():
        for u in range(BLOCK):
            seed_local(u).start()

    @pl.when(band == 4)
    def _():
        for u in range(BLOCK):
            seed(u, 0).start()

    @pl.when(is_root)
    def _():
        for steps in ((2, -2), (1, -1)):
            for u in range(BLOCK):
                for step in steps:
                    seed(u, step).start()

    for i in range(EARLY):
        direct(i).start()
    for i in range(HALF):
        own(i).start()

    def advance(i):
        cross(i).wait_recv()
        passed(i).start()

        @pl.when(i + WINDOW < HALF)
        def _():
            cross(i + WINDOW).start()

        @pl.when(i + EARLY < HALF)
        def _():
            direct(i + EARLY).start()

    for u in range(BLOCK):
        arrive(u)
    for slab in range(2):
        side(slab).start()
        swap(1 + slab).start()
    for i in range(WINDOW):
        cross(i).start()
    advance(0)
    for slab in range(2):
        side(slab).wait_recv()
        swap(3 - 3 * slab).start()
    for slot in range(4):
        swap(slot).wait_recv()

    weights.wait()
    lane = lax.broadcasted_iota(jnp.int32, (KSTRIP, CZ), 1)
    sub = lax.broadcasted_iota(jnp.int32, (KSTRIP, CZ), 0)

    def stencil(r, carry):
        plane, y = 4 * pair + r // (CY // KSTRIP), sub + KSTRIP * lax.rem(
            r, CY // KSTRIP
        )
        start = SLAB + r * KSTRIP
        centre = []
        for b in range(NB):
            c = block_ref[b, pl.ds(start, KSTRIP), :] * (-occ_ref[weight_rows[b]])
            rolled = {}
            for dz in range(-2, 3):
                if dz == 0:
                    rolled[dz] = c
                else:
                    inside = lane >= dz if dz > 0 else lane < CZ + dz
                    rolled[dz] = jnp.where(
                        inside, pltpu.roll(c, dz % CZ, axis=1), 0.0
                    )
            centre.append(rolled)
        one, nil = jnp.float32(1.0), jnp.float32(0.0)
        for dx, dy in PLANE_OFFSETS:
            there = [
                block_ref[b, pl.ds(start + dx * CY + dy, KSTRIP), :] for b in range(NB)
            ]
            inside_x = jnp.logical_and(plane + dx >= 0, plane + dx < 4 * PAIRS)
            for dz in range(-2, 3):
                if abs(dx) + abs(dy) + abs(dz) > 2:
                    continue
                total = centre[0][dz] * there[0]
                for b in range(1, NB):
                    total = total + centre[b][dz] * there[b]
                if dx == dy == dz == 0:
                    sides = jnp.where(plane > 0, one, nil) + jnp.where(
                        plane < 4 * PAIRS - 1, one, nil
                    )
                    count = (
                        sides
                        + jnp.where(y > 0, one, nil)
                        + jnp.where(y < CY - 1, one, nil)
                        + jnp.where(lane > 0, one, nil)
                        + jnp.where(lane < CZ - 1, one, nil)
                    )
                    factor = (36.0 + count) * (1.0 / 216.0)
                else:
                    factor = jnp.float32(coefficient((dx, dy, dz)))
                    if dx:
                        factor = jnp.where(inside_x, factor, nil)
                    if dy:
                        inside_y = y + dy >= 0 if dy < 0 else y + dy < CY
                        factor = jnp.where(inside_y, factor, nil)
                k_ref[INDEX[dx, dy, dz], pl.ds(r * KSTRIP, KSTRIP), :] = total * factor
        return carry

    lax.fori_loop(0, 4 * CY // KSTRIP, stencil, 0)

    def orbital(i, carry):
        @pl.when(i + 1 < HALF)
        def _():
            advance(i + 1)

        own(i).wait()
        direct(i).wait_recv()
        passed(i).wait_recv()

        def strip(r, inner):
            start = SLAB + r * STRIP
            sums = {}
            for dx, dy in PLANE_OFFSETS:
                there = w_ref[i, pl.ds(start + dx * CY + dy, STRIP), :]
                for dz in range(-2, 3):
                    if abs(dx) + abs(dy) + abs(dz) <= 2:
                        term = k_ref[INDEX[dx, dy, dz], pl.ds(r * STRIP, STRIP), :] * there
                        sums[dz] = term if dz not in sums else sums[dz] + term
            result = sums[0]
            for dz in (-2, -1, 1, 2):
                result = result + pltpu.roll(sums[dz], -dz % CZ, axis=1)
            out_ref[i, pl.ds(r * STRIP, STRIP), :] = result
            return inner

        def planes(slab):
            first = slab * (SLAB // STRIP)
            lax.fori_loop(first, first + SLAB // STRIP, strip, 0)

        planes(1 - half)
        back(i).start()
        planes(half)
        keep(i).start()
        return carry

    lax.fori_loop(0, HALF, orbital, 0)

    def finish(i, carry):
        cross(i).wait_send()
        direct(i).wait_send()
        passed(i).wait_send()
        keep(i).wait()
        back(i).wait()
        return carry

    lax.fori_loop(0, HALF, finish, 0)
    for slab in range(2):
        side(slab).wait_send()
    for slot in range(4):
        swap(slot).wait_send()

    @pl.when(is_relay)
    def _():
        for u in range(BLOCK):
            relays(u, lambda copy: copy.wait_send())

    @pl.when(band == 4)
    def _():
        for u in range(BLOCK):
            seed(u, 0).wait_send()

    @pl.when(is_root)
    def _():
        for u in range(BLOCK):
            for step in RELAYS:
                seed(u, step).wait_send()


def per_device(orbitals, occupations):
    count, planes = orbitals.shape[:2]
    groups = lax.axis_size("band")
    weight_rows = [
        s * (groups // STEPS) * count + s * BLOCK + b
        for s in range(STEPS)
        for b in range(BLOCK)
    ]
    dma = pltpu.SemaphoreType.DMA
    out = pl.pallas_call(
        functools.partial(kernel, weight_rows),
        name="exchange",
        out_shape=jax.ShapeDtypeStruct((count, planes * CY, CZ), jnp.float32),
        in_specs=[
            pl.BlockSpec(memory_space=pltpu.HBM),
            pl.BlockSpec(memory_space=pltpu.HBM),
        ],
        out_specs=pl.BlockSpec(memory_space=pl.ANY),
        scratch_shapes=[
            pltpu.SMEM(occupations.shape, jnp.float32),
            dma,
            pltpu.VMEM((HALF, 4 * SLAB, CZ), jnp.float32),
            pltpu.VMEM((NB, 4 * SLAB, CZ), jnp.float32),
            pltpu.VMEM((len(OFFSETS), 2 * SLAB, CZ), jnp.float32),
            pltpu.VMEM((HALF, 2 * SLAB, CZ), jnp.float32),
            dma((HALF,)),
            dma((HALF,)),
            dma((HALF,)),
            dma((HALF,)),
            dma((HALF,)),
            dma((HALF,)),
            dma((HALF,)),
            dma((HALF,)),
            dma((HALF,)),
            dma((HALF,)),
            dma((BLOCK,)),
            dma((BLOCK, len(SEEDS))),
            dma((BLOCK, len(RELAYS))),
            dma((2, BLOCK)),
            dma((2,)),
            dma((2,)),
            dma((4,)),
            dma((4,)),
        ],
        compiler_params=pltpu.CompilerParams(
            collective_id=0, has_side_effects=True, vmem_limit_bytes=40 * 2**20
        ),
    )(
        pltpu.with_memory_space_constraint(occupations, pltpu.HBM),
        pltpu.with_memory_space_constraint(
            orbitals.reshape(count, planes * CY, CZ), pltpu.HBM
        ),
    )
    return out.reshape(orbitals.shape)


def solution(mesh):
    in_specs = (P("band", "dom", None, None), P())
    out_specs = P("band", "dom", None, None)
    return jax.shard_map(
        per_device, mesh=mesh, in_specs=in_specs, out_specs=out_specs, check_vma=False
    )
```

```python
import functools

import jax
import jax.numpy as jnp
from jax import lax
from jax.experimental import pallas as pl
from jax.experimental.pallas import tpu as pltpu
from jax.sharding import PartitionSpec as P

MESH = pl.DeviceIdType.MESH

BLOCK = 2
STEPS = 2
NB = BLOCK * STEPS
CY = 128
CZ = 128
SLAB = 2 * CY
PAIRS = 32
HALF = 6
STRIP = 128
KSTRIP = 64
EARLY = 3
RELAYS = (1, 2, -1, -2)
SEEDS = (*RELAYS, 0)
WINDOW = 3

PLANE_OFFSETS = [
    (dx, dy) for dx in range(-2, 3) for dy in range(-2, 3) if abs(dx) + abs(dy) <= 2
]
OFFSETS = [
    (dx, dy, dz)
    for dx, dy in PLANE_OFFSETS
    for dz in range(-2, 3)
    if abs(dx) + abs(dy) + abs(dz) <= 2
]
INDEX = {offset: k for k, offset in enumerate(OFFSETS)}


def coefficient(offset):
    steps = sum(abs(d) for d in offset)
    if steps == 1:
        return 1.0 / 36.0
    return (1.0 if 2 in map(abs, offset) else 2.0) / 216.0


def kernel(
    weight_rows,
    occ_hbm,
    x_ref,
    o_ref,
    occ_ref,
    occ_sem,
    w_ref,
    block_ref,
    k_ref,
    out_ref,
    own_sem,
    cross_send,
    cross_recv,
    direct_send,
    direct_recv,
    pass_send,
    pass_recv,
    back_send,
    back_recv,
    keep_sem,
    root_own,
    seed_send,
    relay_send,
    root_recv,
    side_send,
    side_recv,
    core_send,
    core_recv,
):
    band, dom = lax.axis_index("band"), lax.axis_index("dom")
    core, z_lo = lax.rem(band, 2), band // 2
    half, pair = lax.rem(dom, 2), dom // 2
    right_pair = lax.rem(pair + 1, PAIRS)
    left_pair = lax.rem(pair + PAIRS - 1, PAIRS)
    partner = (band, dom + 1 - 2 * half)
    sibling = (band + 1 - 2 * core, dom)
    right = (band, 2 * right_pair + half)
    left = (band, 2 * left_pair + half)
    ahead = (band, 2 * jnp.where(half == 0, right_pair, left_pair) + half)
    behind = (band, 2 * jnp.where(half == 0, left_pair, right_pair) + half)
    z = 4 * half + z_lo

    def chip(step, c):
        k = lax.rem(z + step + 8, 8)
        return (2 * lax.rem(k, 4) + c, 2 * pair + k // 4)

    def rows(slab):
        return pl.ds(pl.multiple_of(slab * SLAB, SLAB), SLAB)

    def remote(src, dst, send, recv, device):
        return pltpu.make_async_remote_copy(
            src_ref=src,
            dst_ref=dst,
            send_sem=send,
            recv_sem=recv,
            device_id=device,
            device_id_type=MESH,
        )

    def own(i):
        return pltpu.make_async_copy(
            x_ref.at[HALF * half + i], w_ref.at[i, rows(1 + half)], own_sem.at[i]
        )

    def cross(i):
        return remote(
            x_ref.at[HALF * (1 - half) + i],
            w_ref.at[i, rows(1 + half)],
            cross_send.at[i],
            cross_recv.at[i],
            partner,
        )

    def direct(i):
        return remote(
            x_ref.at[HALF * half + i],
            w_ref.at[i, rows(3 - 3 * half)],
            direct_send.at[i],
            direct_recv.at[i],
            behind,
        )

    def passed(i):
        return remote(
            w_ref.at[i, rows(2 - half)],
            w_ref.at[i, rows(3 * half)],
            pass_send.at[i],
            pass_recv.at[i],
            ahead,
        )

    def back(i):
        return remote(
            out_ref.at[i, rows(1 - half)],
            o_ref.at[HALF * half + i],
            back_send.at[i],
            back_recv.at[i],
            partner,
        )

    def keep(i):
        return pltpu.make_async_copy(
            out_ref.at[i, rows(half)], o_ref.at[HALF * half + i], keep_sem.at[i]
        )

    mine = pl.ds(BLOCK * core, BLOCK)
    is_root = jnp.logical_or(band == 0, band == 4)
    group = band // 4
    is_relay = jnp.logical_and(lax.rem(z, 2) == 0, lax.rem(z, 4) != 2 * core)
    before = lax.rem(z + 6, 8) // 4

    def seed(u, step):
        return remote(
            x_ref.at[BLOCK * group + u],
            block_ref.at[BLOCK * group + u, rows(1 + half)],
            seed_send.at[u, SEEDS.index(step)],
            root_recv.at[half, u],
            sibling if step == 0 else chip(step, group),
        )

    def seed_local(u):
        return pltpu.make_async_copy(
            x_ref.at[u], block_ref.at[u, rows(1 + half)], root_own.at[u]
        )

    def relay(slab, u, step):
        part = block_ref.at[BLOCK * core + u, rows(1 + slab)]
        return remote(
            part,
            part,
            relay_send.at[u, RELAYS.index(step)],
            root_recv.at[slab, u],
            chip(step, core),
        )

    def relays(u, act):
        if u == 0:
            act(relay(before, u, 2))
        else:
            act(relay(1 - before, u, -2))
        act(relay(1 - before, u, -1))
        act(relay(before, u, 1))

    def arrive(u):
        @pl.when(is_relay)
        def _():
            for slab in range(2):
                relay(slab, u, 1).wait_recv()
            relays(u, lambda copy: copy.start())

        for slab in range(2):
            local = jnp.logical_and(band == 0, half == slab)

            @pl.when(local)
            def _():
                seed_local(u).wait()

            @pl.when(jnp.logical_not(jnp.logical_or(local, is_relay)))
            def _():
                relay(slab, u, 1).wait_recv()

    def side(slab):
        return remote(
            block_ref.at[mine, rows(1 + slab)],
            block_ref.at[mine, rows(3 - 3 * slab)],
            side_send.at[slab],
            side_recv.at[slab],
            (band, 2 * jnp.where(slab == 0, left_pair, right_pair) + half),
        )

    def swap(slot):
        part = block_ref.at[mine, rows(slot)]
        return remote(part, part, core_send.at[slot], core_recv.at[slot], sibling)

    weights = pltpu.make_async_copy(occ_hbm, occ_ref, occ_sem)
    weights.start()

    barrier = pltpu.get_barrier_semaphore()
    near = [chip(step, c) for step in RELAYS for c in range(2)]
    for device in (partner, sibling, left, right, *near):
        pl.semaphore_signal(barrier, inc=1, device_id=device, device_id_type=MESH)
    pl.semaphore_wait(barrier, 4 + len(near))

    @pl.when(band == 0)
    def _():
        for u in range(BLOCK):
            seed_local(u).start()

    @pl.when(band == 4)
    def _():
        for u in range(BLOCK):
            seed(u, 0).start()

    @pl.when(is_root)
    def _():
        for steps in ((2, -2), (1, -1)):
            for u in range(BLOCK):
                for step in steps:
                    seed(u, step).start()

    for i in range(EARLY):
        direct(i).start()
    for i in range(HALF):
        own(i).start()

    def advance(i):
        cross(i).wait_recv()
        passed(i).start()

        @pl.when(i + WINDOW < HALF)
        def _():
            cross(i + WINDOW).start()

        @pl.when(i + EARLY < HALF)
        def _():
            direct(i + EARLY).start()

    at_root = lax.rem(z, 4) == 2 * core
    arrive(0)

    @pl.when(at_root)
    def _():
        for i in range(3):
            cross(i).start()

    arrive(1)
    for slab in range(2):
        side(slab).start()
        swap(1 + slab).start()

    @pl.when(jnp.logical_not(at_root))
    def _():
        for i in range(3):
            cross(i).start()

    for i in range(3, WINDOW):
        cross(i).start()
    advance(0)
    for slab in range(2):
        side(slab).wait_recv()
        swap(3 - 3 * slab).start()
    for slot in range(4):
        swap(slot).wait_recv()

    weights.wait()
    lane = lax.broadcasted_iota(jnp.int32, (KSTRIP, CZ), 1)
    sub = lax.broadcasted_iota(jnp.int32, (KSTRIP, CZ), 0)

    def stencil(r, carry):
        plane, y = 4 * pair + r // (CY // KSTRIP), sub + KSTRIP * lax.rem(
            r, CY // KSTRIP
        )
        start = SLAB + r * KSTRIP
        centre = []
        for b in range(NB):
            c = block_ref[b, pl.ds(start, KSTRIP), :] * (-occ_ref[weight_rows[b]])
            rolled = {}
            for dz in range(-2, 3):
                if dz == 0:
                    rolled[dz] = c
                else:
                    inside = lane >= dz if dz > 0 else lane < CZ + dz
                    rolled[dz] = jnp.where(
                        inside, pltpu.roll(c, dz % CZ, axis=1), 0.0
                    )
            centre.append(rolled)
        one, nil = jnp.float32(1.0), jnp.float32(0.0)
        for dx, dy in PLANE_OFFSETS:
            there = [
                block_ref[b, pl.ds(start + dx * CY + dy, KSTRIP), :] for b in range(NB)
            ]
            inside_x = jnp.logical_and(plane + dx >= 0, plane + dx < 4 * PAIRS)
            for dz in range(-2, 3):
                if abs(dx) + abs(dy) + abs(dz) > 2:
                    continue
                total = centre[0][dz] * there[0]
                for b in range(1, NB):
                    total = total + centre[b][dz] * there[b]
                if dx == dy == dz == 0:
                    sides = jnp.where(plane > 0, one, nil) + jnp.where(
                        plane < 4 * PAIRS - 1, one, nil
                    )
                    count = (
                        sides
                        + jnp.where(y > 0, one, nil)
                        + jnp.where(y < CY - 1, one, nil)
                        + jnp.where(lane > 0, one, nil)
                        + jnp.where(lane < CZ - 1, one, nil)
                    )
                    factor = (36.0 + count) * (1.0 / 216.0)
                else:
                    factor = jnp.float32(coefficient((dx, dy, dz)))
                    if dx:
                        factor = jnp.where(inside_x, factor, nil)
                    if dy:
                        inside_y = y + dy >= 0 if dy < 0 else y + dy < CY
                        factor = jnp.where(inside_y, factor, nil)
                k_ref[INDEX[dx, dy, dz], pl.ds(r * KSTRIP, KSTRIP), :] = total * factor
        return carry

    lax.fori_loop(0, 4 * CY // KSTRIP, stencil, 0)

    def orbital(i, carry):
        @pl.when(i + 1 < HALF)
        def _():
            advance(i + 1)

        own(i).wait()
        direct(i).wait_recv()
        passed(i).wait_recv()

        def strip(r, inner):
            start = SLAB + r * STRIP
            sums = {}
            for dx, dy in PLANE_OFFSETS:
                there = w_ref[i, pl.ds(start + dx * CY + dy, STRIP), :]
                for dz in range(-2, 3):
                    if abs(dx) + abs(dy) + abs(dz) <= 2:
                        term = k_ref[INDEX[dx, dy, dz], pl.ds(r * STRIP, STRIP), :] * there
                        sums[dz] = term if dz not in sums else sums[dz] + term
            result = sums[0]
            for dz in (-2, -1, 1, 2):
                result = result + pltpu.roll(sums[dz], -dz % CZ, axis=1)
            out_ref[i, pl.ds(r * STRIP, STRIP), :] = result
            return inner

        def planes(slab):
            first = slab * (SLAB // STRIP)
            lax.fori_loop(first, first + SLAB // STRIP, strip, 0)

        planes(1 - half)
        back(i).start()
        planes(half)
        keep(i).start()
        return carry

    lax.fori_loop(0, HALF, orbital, 0)

    def finish(i, carry):
        cross(i).wait_send()
        direct(i).wait_send()
        passed(i).wait_send()
        keep(i).wait()
        back(i).wait()
        return carry

    lax.fori_loop(0, HALF, finish, 0)
    for slab in range(2):
        side(slab).wait_send()
    for slot in range(4):
        swap(slot).wait_send()

    @pl.when(is_relay)
    def _():
        for u in range(BLOCK):
            relays(u, lambda copy: copy.wait_send())

    @pl.when(band == 4)
    def _():
        for u in range(BLOCK):
            seed(u, 0).wait_send()

    @pl.when(is_root)
    def _():
        for u in range(BLOCK):
            for step in RELAYS:
                seed(u, step).wait_send()


def per_device(orbitals, occupations):
    count, planes = orbitals.shape[:2]
    groups = lax.axis_size("band")
    weight_rows = [
        s * (groups // STEPS) * count + s * BLOCK + b
        for s in range(STEPS)
        for b in range(BLOCK)
    ]
    dma = pltpu.SemaphoreType.DMA
    out = pl.pallas_call(
        functools.partial(kernel, weight_rows),
        name="exchange",
        out_shape=jax.ShapeDtypeStruct((count, planes * CY, CZ), jnp.float32),
        in_specs=[
            pl.BlockSpec(memory_space=pltpu.HBM),
            pl.BlockSpec(memory_space=pltpu.HBM),
        ],
        out_specs=pl.BlockSpec(memory_space=pl.ANY),
        scratch_shapes=[
            pltpu.SMEM(occupations.shape, jnp.float32),
            dma,
            pltpu.VMEM((HALF, 4 * SLAB, CZ), jnp.float32),
            pltpu.VMEM((NB, 4 * SLAB, CZ), jnp.float32),
            pltpu.VMEM((len(OFFSETS), 2 * SLAB, CZ), jnp.float32),
            pltpu.VMEM((HALF, 2 * SLAB, CZ), jnp.float32),
            dma((HALF,)),
            dma((HALF,)),
            dma((HALF,)),
            dma((HALF,)),
            dma((HALF,)),
            dma((HALF,)),
            dma((HALF,)),
            dma((HALF,)),
            dma((HALF,)),
            dma((HALF,)),
            dma((BLOCK,)),
            dma((BLOCK, len(SEEDS))),
            dma((BLOCK, len(RELAYS))),
            dma((2, BLOCK)),
            dma((2,)),
            dma((2,)),
            dma((4,)),
            dma((4,)),
        ],
        compiler_params=pltpu.CompilerParams(
            collective_id=0, has_side_effects=True, vmem_limit_bytes=40 * 2**20
        ),
    )(
        pltpu.with_memory_space_constraint(occupations, pltpu.HBM),
        pltpu.with_memory_space_constraint(
            orbitals.reshape(count, planes * CY, CZ), pltpu.HBM
        ),
    )
    return out.reshape(orbitals.shape)


def solution(mesh):
    in_specs = (P("band", "dom", None, None), P())
    out_specs = P("band", "dom", None, None)
    return jax.shard_map(
        per_device, mesh=mesh, in_specs=in_specs, out_specs=out_specs, check_vma=False
    )
```
